256 devices in a mesh: val: 16 (over y_hi, x, core), cond: 16 (over y_lo, z).
Axes of the slice: x: 4, y: 4 (y_hi: 2, y_lo: 2; y = y_hi * 2 + y_lo), z: 8, core: 2. Of those that a mesh axis runs over, the one named last changes fastest.
Arguments:
- trial: bfloat16 [256, 65536], P('val', 'cond'), may hold values from -6 to 6
- pair_cond: bfloat16 [80, 1024, 1024], P('val', 'cond'), may hold values from -0.1875 to 0.1875
- pair_val: bfloat16 [256, 20480], P(None, 'val'), may hold values from -0.0625 to 0.0625
Outputs:
- applied: bfloat16 [256, 65536], P('val', 'cond')
The draws below stay inside these ranges and needn't reach their ends.
All inputs are finite; a program needn't handle non-finite values.
Results may differ from the reference program's by a relative error of at most 0.0049.
Values may be sent and summed in bfloat16 or wider, within the bound.
A program may use at most 128 MiB of HBM per device.

```python
import jax
import jax.numpy as jnp
from jax import lax

V = 256
C = 1024
S = 64
G = 80


def with_spikes(values, rng, source, target, parts, factor):
    def block_of(dim):
        return (jnp.arange(values.shape[dim]) // (values.shape[dim] // parts)).reshape((-1,) + (1,) * (values.ndim - 1 - dim))

    first = jax.random.permutation(rng, parts)[block_of(target)]
    other_side = (block_of(target) + parts // 2) % parts
    return jnp.where((block_of(source) == first) | (block_of(source) == other_side), factor * values, values)


def shard_levels(own_key, extent, pieces, low, largest):
    def one(dim, blocks):
        draws = jax.random.uniform(jax.random.fold_in(jax.random.fold_in(own_key, 6), dim), (blocks,), jnp.float32, low / len(pieces), largest / len(pieces))
        return jnp.repeat(jnp.exp(draws), extent[dim] // blocks).reshape((-1,) + (1,) * (len(extent) - dim - 1))

    factor_of = one(*pieces[0])
    for cut in pieces[1:]:
        factor_of = factor_of * one(*cut)
    return factor_of


def normal_values(key, shape, scale, limit, cuts=(), kind=jnp.bfloat16):
    loudness = shard_levels(key, shape, cuts, -0.22, 0.18) if cuts else 1.0
    values = jax.random.normal(key, shape, jnp.float32) * scale * loudness
    return jnp.minimum(jnp.maximum(values, -limit), limit).astype(kind)


def noise_with(key, extent, width, most, split, heavy, kind=jnp.bfloat16):
    values = width * jax.random.normal(key, extent, jnp.float32)
    if split:
        values = values * shard_levels(key, extent, split, -0.22, 0.18)
    return jnp.clip(with_spikes(values, jax.random.fold_in(key, 3), *heavy), -most, most).astype(kind)


def setup_inputs(seed: int = 0) -> dict:
    streams_of = jax.random.split(jax.random.key(seed), 4)
    return {
        "trial": normal_values(streams_of[0], (V, C * S), 1.0, 6.0, ((0, 16), (1, 16))),
        "pair_cond": normal_values(streams_of[1], (G, C, C), C ** -0.5, 0.1875, ((0, 16), (1, 16))),
        "pair_val": noise_with(streams_of[2], (V, V * G), (V * G) ** -0.5, 0.0625, ((1, 16),), (1, 0, 16, 2.0)),
    }


def reference(trial, pair_cond, pair_val):
    trial_wide = trial.astype(jnp.float32).reshape(V, C, S)
    val_wide = pair_val.reshape(V, V, G)

    def advance(total, index):
        cond_slab = lax.dynamic_index_in_dim(pair_cond, index, 0, keepdims=False).astype(jnp.float32)
        val_slab = lax.dynamic_index_in_dim(val_wide, index, 2, keepdims=False).astype(jnp.float32)
        inner = jnp.einsum("cd,wds->wcs", cond_slab, trial_wide).astype(jnp.bfloat16)
        total = total + jnp.einsum("vw,wcs->vcs", val_slab, inner.astype(jnp.float32))
        return total, None

    start = jnp.zeros((V, C, S), jnp.float32)
    total, _ = lax.scan(advance, start, jnp.arange(G, dtype=jnp.int32))
    return total.reshape(V, C * S).astype(jnp.bfloat16)
```

```python
import jax
import jax.numpy as jnp
from jax import lax
from jax.experimental import pallas as pl
from jax.experimental.pallas import tpu as pltpu
from jax.sharding import PartitionSpec as P

MESH = pl.DeviceIdType.MESH
F32, BF16 = jnp.float32, jnp.bfloat16
NQ = 4
NJ = 4
Z = 8


def device(x, y, z, core):
    x, y, z = lax.rem(x + 4, 4), lax.rem(y + 4, 4), lax.rem(z + Z, Z)
    return {"val": (y // 2) * 8 + x * 2 + core, "cond": lax.rem(y, 2) * Z + z}


def kernel(trial_ref, pc_hbm, pv_ref, out_ref, pcb, tb, pvs, pvall, perm, bs, ts, ys, xs, acc,
           rbuf, sbuf, obuf, loc_sem, pc_s, pc_r, sib_s, sib_r, ty_s, ty_r, tz_s, tz_r, pv_s, pv_r,
           d2_s, d2_r, o_s, o_r):
    val, cond = lax.axis_index("val"), lax.axis_index("cond")
    yh, yl, z = val // 8, cond // Z, lax.rem(cond, Z)
    x, core, y = lax.rem(val, 8) // 2, lax.rem(val, 2), (val // 8) * 2 + cond // Z
    sibling = device(x, y, z, 1 - core)
    xpeer = [device(x + d, y, z, core) for d in (1, 2, 3)]
    ypeer = [device(x, y + d, z, core) for d in (1, 2, 3)]
    zpeer = [device(x, y, z + 1, core), device(x, y, z - 1, core)]
    opeer = xpeer + [device(x + d, y + 2, z, core) for d in (0, 1, 2, 3)]
    partners = [sibling] + xpeer + ypeer + zpeer + opeer[4:]

    barrier = pltpu.get_barrier_semaphore()
    for p in partners:
        pl.semaphore_signal(barrier, 1, device_id=p, device_id_type=MESH)
    pl.semaphore_wait(barrier, len(partners))

    sent = []

    def send(src, dst, s, r, to):
        cp = pltpu.make_async_remote_copy(src, dst, s, r, device_id=to, device_id_type=MESH)
        cp.start()
        sent.append(cp)
        return cp

    pc_cp, loc_cp = [], []
    for j in range(NJ):
        src = pc_hbm.at[:, pl.ds(j * 16, 16), :]
        cp = pltpu.make_async_copy(src, pcb.at[j, x, core], loc_sem.at[j])
        cp.start()
        loc_cp.append(cp)
        pc_cp.append([send(src, pcb.at[j, x, core], pc_s.at[j, d], pc_r.at[j, d], xpeer[d]) for d in (0, 2, 1)])

    lane = lax.broadcasted_iota(jnp.int32, (32, 128), 1) < 64
    for i in range(32):
        bs[pl.ds(i, 16, stride=32), :] = trial_ref[:, i * 128:(i + 1) * 128].astype(F32)
    ty_cp = []
    for q in range(NQ):
        for half in range(2):
            w = (q * 2 + half) * 2
            b0, b1 = bs[w * 32:w * 32 + 32, :], bs[w * 32 + 32:w * 32 + 64, :]
            ts[pl.ds(0, 32, stride=2), :] = jnp.where(lane, b0, pltpu.roll(b1, 64, 1))
            ts[pl.ds(1, 32, stride=2), :] = jnp.where(lane, pltpu.roll(b0, 64, 1), b1)
            tb[q, yh, yl, z, :, half * 128:half * 128 + 128] = ts[...].astype(BF16)
        mine = tb.at[q, yh, yl, z]
        ty_cp.append([send(mine, mine, ty_s.at[q, d], ty_r.at[q, d], ypeer[d]) for d in (0, 2, 1)])

    def select(h):
        row = lax.broadcasted_iota(jnp.int32, (1280, 640), 0)
        col = lax.broadcasted_iota(jnp.int32, (1280, 640), 1)
        perm[...] = jnp.where(row == col + 40 * ((col * 1639) >> 16) + 40 * h, 1.0, 0.0).astype(BF16)
        return jnp.dot(pv_ref[...], perm[...], preferred_element_type=F32).astype(BF16)

    pvs[...] = select(1 - yh)
    pv_cp = send(pvs, pvall.at[yh], pv_s, pv_r, ypeer[1])
    pvall[yh] = select(yh)

    tz_cp = {}

    def e(q, s):
        if s == 1:
            for cp in ty_cp[q]:
                cp.wait_recv()
        else:
            for cp in tz_cp[q, s - 1]:
                cp.wait_recv()
        near, far = lax.rem(z - (s - 1) + Z, Z), lax.rem(z + s - 1, Z)
        if s < 4:
            a, b = tb.at[q, :, :, near], tb.at[q, :, :, far]
        else:
            a, b = tb.at[q, 0, :, near], tb.at[q, 1, :, far]
        tz_cp[q, s] = [send(a, a, tz_s.at[q, s - 1, 0], tz_r.at[q, s - 1, 0], zpeer[0]),
                       send(b, b, tz_s.at[q, s - 1, 1], tz_r.at[q, s - 1, 1], zpeer[1])]

    def f(q):
        for cp in tz_cp[q, 4]:
            cp.wait_recv()

    sib_cp = {}

    def p(j):
        loc_cp[j].wait()
        for cp in pc_cp[j]:
            cp.wait_recv()
        sib_cp[j] = send(pcb.at[j, :, core], pcb.at[j, :, core], sib_s.at[j], sib_r.at[j], sibling)

    low = lax.broadcasted_iota(jnp.int32, (40, 128), 1) < 64

    def r(q, j):
        if q == 0:
            sib_cp[j].wait_recv()
        lhs = pcb[j].reshape(640, 1024)
        for h in range(2):
            rhs = tb[q, h].reshape(1024, 256)
            prod = jnp.dot(lhs, rhs, preferred_element_type=F32)
            ys[h, 0] = prod[:, :128]
            ys[h, 1] = prod[:, 128:]
            for wp in range(2):
                for cp in range(8):
                    c0 = ys[h, wp, pl.ds(2 * cp, 40, stride=16), :]
                    c1 = ys[h, wp, pl.ds(2 * cp + 1, 40, stride=16), :]
                    w0 = jnp.where(low, c0, pltpu.roll(c1, 64, 1))
                    w1 = jnp.where(low, pltpu.roll(c0, 64, 1), c1)
                    xs[h, wp * 80:wp * 80 + 80, cp * 128:cp * 128 + 128] = jnp.concatenate([w0, w1], 0).astype(BF16)
        total = None
        for h in range(2):
            t = jnp.dot(pvall[h, :, q * 160:q * 160 + 160], xs[h], preferred_element_type=F32)
            total = t if total is None else total + t
        total = total.reshape(8, 2, 16, 1024)
        if q == 0:
            acc[j] = total
        else:
            acc[j] += total

    d2_cp = {}

    def d(j):
        d2_cp[j] = send(acc.at[j, :, 1 - core], rbuf.at[j], d2_s.at[j], d2_r.at[j], sibling)

    o_cp = {}
    who = [lax.rem(x + dx, 4) + 4 * yh for dx in (1, 2, 3)] + [lax.rem(x + dx, 4) + 4 * (1 - yh) for dx in (0, 1, 2, 3)]
    me = x + 4 * yh

    def s(j):
        d2_cp[j].wait_recv()
        sbuf[j] = (acc[j, :, core] + rbuf[j]).astype(BF16)
        o_cp[j] = [send(sbuf.at[j, who[i]], obuf.at[j, i], o_s.at[j, i], o_r.at[j, i], opeer[i]) for i in range(7)]

    def o(j):
        for cp in o_cp[j]:
            cp.wait_recv()
        total = acc[j, me, core] + rbuf[j, me]
        for i in range(7):
            total = total + obuf[j, i].astype(F32)
        out_ref[:, j * 1024:(j + 1) * 1024] = total.astype(BF16)

    e(0, 1)
    e(1, 1)
    e(0, 2)
    e(1, 2)
    p(0)
    e(0, 3)
    e(1, 3)
    e(0, 4)
    e(2, 1)
    e(1, 4)
    p(1)
    f(0)
    e(3, 1)
    f(1)
    pv_cp.wait_recv()
    r(0, 0)
    e(2, 2)
    p(2)
    r(0, 1)
    e(3, 2)
    p(3)
    r(0, 2)
    e(2, 3)
    r(0, 3)
    r(1, 0)
    e(3, 3)
    r(1, 1)
    r(1, 2)
    e(2, 4)
    r(1, 3)
    e(3, 4)
    f(2)
    for j in range(NJ):
        r(2, j)
    f(3)
    for j in range(NJ):
        r(3, j)
        d(j)
        if j:
            s(j - 1)
    s(NJ - 1)
    for j in range(NJ):
        o(j)
    for cp in sent:
        cp.wait_send()


def body(trial, pair_cond, pair_val):
    dma = pltpu.SemaphoreType.DMA
    vmem = pl.BlockSpec(memory_space=pltpu.VMEM)
    return pl.pallas_call(
        kernel,
        out_shape=jax.ShapeDtypeStruct((16, 4096), BF16),
        in_specs=[vmem, pl.BlockSpec(memory_space=pl.ANY), vmem],
        out_specs=vmem,
        scratch_shapes=[
            pltpu.VMEM((NJ, 4, 2, 5, 16, 1024), BF16),
            pltpu.VMEM((NQ, 2, 2, Z, 64, 256), BF16),
            pltpu.VMEM((256, 640), BF16),
            pltpu.VMEM((2, 256, 640), BF16),
            pltpu.VMEM((1280, 640), BF16),
            pltpu.VMEM((512, 128), F32),
            pltpu.VMEM((64, 128), F32),
            pltpu.VMEM((2, 2, 640, 128), F32),
            pltpu.VMEM((2, 160, 1024), BF16),
            pltpu.VMEM((NJ, 8, 2, 16, 1024), F32),
            pltpu.VMEM((NJ, 8, 16, 1024), F32),
            pltpu.VMEM((NJ, 8, 16, 1024), BF16),
            pltpu.VMEM((NJ, 7, 16, 1024), BF16),
            dma((NJ,)), dma((NJ, 3)), dma((NJ, 3)), dma((NJ,)), dma((NJ,)),
            dma((NQ, 3)), dma((NQ, 3)), dma((NQ, 4, 2)), dma((NQ, 4, 2)), dma(()), dma(()),
            dma((NJ,)), dma((NJ,)), dma((NJ, 7)), dma((NJ, 7)),
        ],
        compiler_params=pltpu.CompilerParams(
            collective_id=0, has_side_effects=True, vmem_limit_bytes=56 << 20
        ),
    )(trial, pair_cond, pair_val)


def solution(mesh):
    in_specs = (P("val", "cond"), P("val", "cond", None), P(None, "val"))
    return jax.shard_map(body, mesh=mesh, in_specs=in_specs, out_specs=P("val", "cond"), check_vma=False)
```

```python
import jax
import jax.numpy as jnp
from jax import lax
from jax.experimental import pallas as pl
from jax.experimental.pallas import tpu as pltpu
from jax.sharding import PartitionSpec as P

MESH = pl.DeviceIdType.MESH
F32, BF16 = jnp.float32, jnp.bfloat16
NQ = 4
NJ = 4
Z = 8


def device(x, y, z, core):
    x, y, z = lax.rem(x + 4, 4), lax.rem(y + 4, 4), lax.rem(z + Z, Z)
    return {"val": (y // 2) * 8 + x * 2 + core, "cond": lax.rem(y, 2) * Z + z}


def kernel(trial_ref, pc_hbm, pv_ref, out_ref, pcb, tb, pvs, pvall, perm, bs, ts, ys, xs, acc,
           rbuf, sbuf, obuf, loc_sem, pc_s, pc_r, sib_s, sib_r, ty_s, ty_r, tz_s, tz_r, pv_s, pv_r,
           d2_s, d2_r, o_s, o_r):
    val, cond = lax.axis_index("val"), lax.axis_index("cond")
    yh, yl, z = val // 8, cond // Z, lax.rem(cond, Z)
    x, core, y = lax.rem(val, 8) // 2, lax.rem(val, 2), (val // 8) * 2 + cond // Z
    sibling = device(x, y, z, 1 - core)
    xpeer = [device(x + d, y, z, core) for d in (1, 2, 3)]
    ypeer = [device(x, y + d, z, core) for d in (1, 2, 3)]
    zpeer = [device(x, y, z + d, core) for d in (1, -1, 2, -2)]
    opeer = xpeer + [device(x + d, y + 2, z, core) for d in (0, 1, 2, 3)]
    partners = [sibling] + xpeer + ypeer + zpeer + opeer[4:]

    barrier = pltpu.get_barrier_semaphore()
    for p in partners:
        pl.semaphore_signal(barrier, 1, device_id=p, device_id_type=MESH)
    sent = []

    def send(src, dst, s, r, to):
        cp = pltpu.make_async_remote_copy(src, dst, s, r, device_id=to, device_id_type=MESH)
        cp.start()
        sent.append(cp)
        return cp

    lane = lax.broadcasted_iota(jnp.int32, (32, 128), 1) < 64
    for i in range(32):
        bs[pl.ds(i, 16, stride=32), :] = trial_ref[:, i * 128:(i + 1) * 128].astype(F32)
    for q in range(NQ):
        for half in range(2):
            w = (q * 2 + half) * 2
            b0, b1 = bs[w * 32:w * 32 + 32, :], bs[w * 32 + 32:w * 32 + 64, :]
            ts[pl.ds(0, 32, stride=2), :] = jnp.where(lane, b0, pltpu.roll(b1, 64, 1))
            ts[pl.ds(1, 32, stride=2), :] = jnp.where(lane, pltpu.roll(b0, 64, 1), b1)
            tb[q, yh, yl, z, :, half * 128:half * 128 + 128] = ts[...].astype(BF16)

    def select(h):
        row = lax.broadcasted_iota(jnp.int32, (1280, 640), 0)
        col = lax.broadcasted_iota(jnp.int32, (1280, 640), 1)
        perm[...] = jnp.where(row == col + 40 * ((col * 1639) >> 16) + 40 * h, 1.0, 0.0).astype(BF16)
        return jnp.dot(pv_ref[...], perm[...], preferred_element_type=F32).astype(BF16)

    pvs[...] = select(1 - yh)
    pvall[yh] = select(yh)

    pl.semaphore_wait(barrier, len(partners))

    ty_cp, tz_cp, pc_cp, loc_cp = {}, {}, {}, {}
    both = tb.at[2:4, yh, yl, z]
    tz_cp[2, 1] = [send(both, both, tz_s.at[2, 0, i], tz_r.at[2, 0, i], zpeer[i]) for i in (0, 1, 2, 3)]
    for q in range(2):
        mine = tb.at[q, yh, yl, z]
        ty_cp[q] = [send(mine, mine, ty_s.at[q, d], ty_r.at[q, d], ypeer[d]) for d in (0, 2, 1)]
    for j in range(NJ):
        src = pc_hbm.at[:, pl.ds(j * 16, 16), :]
        loc_cp[j] = pltpu.make_async_copy(src, pcb.at[j, x, core], loc_sem.at[j])
        loc_cp[j].start()
        pc_cp[j] = [send(src, pcb.at[j, x, core], pc_s.at[j, d], pc_r.at[j, d], xpeer[d]) for d in (0, 2)]
    pv_cp = send(pvs, pvall.at[yh], pv_s, pv_r, ypeer[1])

    def e(q, s):
        if s == 1:
            for cp in ty_cp[q]:
                cp.wait_recv()
        else:
            for cp in tz_cp[q, s - 1]:
                cp.wait_recv()
        near, far = lax.rem(z - (s - 1) + Z, Z), lax.rem(z + s - 1, Z)
        if s < 4:
            a, b = tb.at[q, :, :, near], tb.at[q, :, :, far]
        else:
            a, b = tb.at[q, 0, :, near], tb.at[q, 1, :, far]
        tz_cp[q, s] = [send(a, a, tz_s.at[q, s - 1, 0], tz_r.at[q, s - 1, 0], zpeer[0]),
                       send(b, b, tz_s.at[q, s - 1, 1], tz_r.at[q, s - 1, 1], zpeer[1])]

    def a():
        for cp in tz_cp[2, 1]:
            cp.wait_recv()
        near, far = lax.rem(z + Z - 2, Z), lax.rem(z + 2, Z)
        n3, f3 = tb.at[2:4, yh, yl, near], tb.at[2:4, yh, yl, far]
        n4, f4 = tb.at[2, yh, yl, near], tb.at[3, yh, yl, far]
        tz_cp[2, 2] = [send(t, t, tz_s.at[2, 1, i], tz_r.at[2, 1, i], zpeer[i]) for i, t in enumerate((n3, f3, n4, f4))]

    def b(q):
        if q == 2:
            for cp in tz_cp[2, 2]:
                cp.wait_recv()
        mine = tb.at[q, yh, yl]
        ty_cp[q] = [send(mine, mine, ty_s.at[q, d], ty_r.at[q, d], ypeer[d]) for d in (0, 2)]

    def c(q):
        for cp in ty_cp[q]:
            cp.wait_recv()
        below, above = lax.rem(y + 3, 4), lax.rem(y + 1, 4)
        lo = tb.at[q, below // 2, lax.rem(below, 2), 0:4]
        hi = tb.at[q, above // 2, lax.rem(above, 2), 4:8]
        ty_cp[q] = [send(lo, lo, ty_s.at[q, 1], ty_r.at[q, 1], ypeer[0]),
                    send(hi, hi, ty_s.at[q, 3], ty_r.at[q, 3], ypeer[2])]

    def g(q):
        for cp in ty_cp[q]:
            cp.wait_recv()

    def f(q):
        for cp in tz_cp[q, 4]:
            cp.wait_recv()

    sib_cp = {}

    def p(j):
        for cp in pc_cp[j]:
            cp.wait_recv()
        lo = pcb.at[j, lax.rem(x + 3, 4), core, :, :, 0:512]
        hi = pcb.at[j, lax.rem(x + 1, 4), core, :, :, 512:1024]
        pc_cp[j] = [send(lo, lo, pc_s.at[j, 1], pc_r.at[j, 1], xpeer[0]),
                    send(hi, hi, pc_s.at[j, 3], pc_r.at[j, 3], xpeer[2])]

    def p2(j):
        loc_cp[j].wait()
        for cp in pc_cp[j]:
            cp.wait_recv()
        sib_cp[j] = send(pcb.at[j, :, core], pcb.at[j, :, core], sib_s.at[j], sib_r.at[j], sibling)

    low = lax.broadcasted_iota(jnp.int32, (40, 128), 1) < 64
    pend, begun = [], set()
    parts = [(i, wp, c) for i in range(2) for wp in range(2) for c in range(8)]

    def relay(u, some):
        pair, h, j, par = u
        for i, wp, c in some:
            c0 = ys[par, i, wp, pl.ds(2 * c, 40, stride=16), :]
            c1 = ys[par, i, wp, pl.ds(2 * c + 1, 40, stride=16), :]
            w0 = jnp.where(low, c0, pltpu.roll(c1, 64, 1))
            w1 = jnp.where(low, pltpu.roll(c0, 64, 1), c1)
            at = i * 160 + wp * 80
            xs[par, at:at + 80, c * 128:c * 128 + 128] = jnp.concatenate([w0, w1], 0).astype(BF16)

    def finish(u):
        pair, h, j, par = u
        t = jnp.dot(pvall[h, :, pair * 320:pair * 320 + 320], xs[par], preferred_element_type=F32)
        t = t.reshape(8, 2, 16, 1024)
        if j not in begun:
            begun.add(j)
            acc[j] = t
        else:
            acc[j] += t

    count = [0]

    def r(pair, h, j):
        par = count[0] % 2
        count[0] += 1
        last = pend.pop() if pend else None
        for i in range(2):
            rhs = tb[pair * 2 + i, h].reshape(1024, 256)
            for m in range(2):
                prod = jnp.dot(pcb[j, 2 * m:2 * m + 2].reshape(320, 1024), rhs, preferred_element_type=F32)
                for wp in range(2):
                    ys[par, i, wp, m * 320:m * 320 + 320] = prod[:, wp * 128:wp * 128 + 128]
                if last:
                    at = (i * 2 + m) * 8
                    relay(last, parts[at:at + 8])
        if last:
            finish(last)
        pend.append((pair, h, j, par))

    def flush():
        u = pend.pop()
        relay(u, parts)
        finish(u)

    d2_cp = {}

    def d(j):
        d2_cp[j] = send(acc.at[j, :, 1 - core], rbuf.at[j], d2_s.at[j], d2_r.at[j], sibling)

    o_cp = {}
    who = [lax.rem(x + dx, 4) + 4 * yh for dx in (1, 2, 3)] + [lax.rem(x + dx, 4) + 4 * (1 - yh) for dx in (0, 1, 2, 3)]
    me = x + 4 * yh

    def s(j):
        d2_cp[j].wait_recv()
        sbuf[j] = (acc[j, :, core] + rbuf[j]).astype(BF16)
        o_cp[j] = [send(sbuf.at[j, who[i]], obuf.at[j, i], o_s.at[j, i], o_r.at[j, i], opeer[i]) for i in range(7)]

    def o(j):
        for cp in o_cp[j]:
            cp.wait_recv()
        total = acc[j, me, core] + rbuf[j, me]
        for i in range(7):
            total = total + obuf[j, i].astype(F32)
        out_ref[:, j * 1024:(j + 1) * 1024] = total.astype(BF16)

    e(0, 1)
    e(1, 1)
    a()
    e(0, 2)
    b(2)
    b(3)
    e(1, 2)
    p(0)
    p(1)
    e(0, 3)
    p(2)
    p(3)
    e(1, 3)
    c(2)
    p2(0)
    e(0, 4)
    p2(1)
    c(3)
    e(1, 4)
    p2(2)
    p2(3)
    pv_cp.wait_recv()
    for j in range(NJ):
        sib_cp[j].wait_recv()
        r(1, yh, j)
    f(0)
    f(1)
    for j in range(NJ):
        r(0, 0, j)
        if j:
            d(j - 1)
        r(0, 1, j)
        if j == 0:
            g(2)
            g(3)
        r(1, 1 - yh, j)
        if j:
            s(j - 1)
    flush()
    d(NJ - 1)
    o(0)
    s(NJ - 1)
    for j in range(1, NJ):
        o(j)
    for cp in sent:
        cp.wait_send()


def body(trial, pair_cond, pair_val):
    dma = pltpu.SemaphoreType.DMA
    vmem = pl.BlockSpec(memory_space=pltpu.VMEM)
    return pl.pallas_call(
        kernel,
        out_shape=jax.ShapeDtypeStruct((16, 4096), BF16),
        in_specs=[vmem, pl.BlockSpec(memory_space=pl.ANY), vmem],
        out_specs=vmem,
        scratch_shapes=[
            pltpu.VMEM((NJ, 4, 2, 5, 16, 1024), BF16),
            pltpu.VMEM((NQ, 2, 2, Z, 64, 256), BF16),
            pltpu.VMEM((256, 640), BF16),
            pltpu.VMEM((2, 256, 640), BF16),
            pltpu.VMEM((1280, 640), BF16),
            pltpu.VMEM((512, 128), F32),
            pltpu.VMEM((64, 128), F32),
            pltpu.VMEM((2, 2, 2, 640, 128), F32),
            pltpu.VMEM((2, 320, 1024), BF16),
            pltpu.VMEM((NJ, 8, 2, 16, 1024), F32),
            pltpu.VMEM((NJ, 8, 16, 1024), F32),
            pltpu.VMEM((NJ, 8, 16, 1024), BF16),
            pltpu.VMEM((NJ, 7, 16, 1024), BF16),
            dma((NJ,)), dma((NJ, 4)), dma((NJ, 4)), dma((NJ,)), dma((NJ,)),
            dma((NQ, 4)), dma((NQ, 4)), dma((NQ, 4, 4)), dma((NQ, 4, 4)), dma(()), dma(()),
            dma((NJ,)), dma((NJ,)), dma((NJ, 7)), dma((NJ, 7)),
        ],
        compiler_params=pltpu.CompilerParams(
            collective_id=0, has_side_effects=True, vmem_limit_bytes=56 << 20
        ),
    )(trial, pair_cond, pair_val)


def solution(mesh):
    in_specs = (P("val", "cond"), P("val", "cond", None), P(None, "val"))
    return jax.shard_map(body, mesh=mesh, in_specs=in_specs, out_specs=P("val", "cond"), check_vma=False)
```

```python
import jax
import jax.numpy as jnp
from jax import lax
from jax.experimental import pallas as pl
from jax.experimental.pallas import tpu as pltpu
from jax.sharding import PartitionSpec as P

MESH = pl.DeviceIdType.MESH
F32, BF16 = jnp.float32, jnp.bfloat16
NQ = 4
NJ = 4
Z = 8


def device(x, y, z, core):
    x, y, z = lax.rem(x + 4, 4), lax.rem(y + 4, 4), lax.rem(z + Z, Z)
    return {"val": (y // 2) * 8 + x * 2 + core, "cond": lax.rem(y, 2) * Z + z}


def kernel(trial_ref, pc_hbm, pv_ref, out_ref, pcb, tb, pvs, pvall, pvc, perm, bs, ts, ys, xs, acc,
           rbuf, sbuf, obuf, loc_sem, pc_s, pc_r, sib_s, sib_r, ty_s, ty_r, tz_s, tz_r, pv_s, pv_r,
           d2_s, d2_r, o_s, o_r):
    val, cond = lax.axis_index("val"), lax.axis_index("cond")
    yh, yl, z = val // 8, cond // Z, lax.rem(cond, Z)
    x, core, y = lax.rem(val, 8) // 2, lax.rem(val, 2), (val // 8) * 2 + cond // Z
    sibling = device(x, y, z, 1 - core)
    xpeer = [device(x + d, y, z, core) for d in (1, 2, 3)]
    ypeer = [device(x, y + d, z, core) for d in (1, 2, 3)]
    zpeer = [device(x, y, z + d, core) for d in (1, -1, 2, -2)]
    opeer = xpeer + [device(x + d, y + 2, z, core) for d in (0, 1, 2, 3)]
    partners = [sibling] + xpeer + ypeer + zpeer

    barrier = pltpu.get_barrier_semaphore()
    for p in partners:
        pl.semaphore_signal(barrier, 1, device_id=p, device_id_type=MESH)
    sent = []

    def send(src, dst, s, r, to):
        cp = pltpu.make_async_remote_copy(src, dst, s, r, device_id=to, device_id_type=MESH)
        cp.start()
        sent.append(cp)
        return cp

    lane = lax.broadcasted_iota(jnp.int32, (32, 128), 1) < 64
    for i in range(32):
        bs[pl.ds(i, 16, stride=32), :] = trial_ref[:, i * 128:(i + 1) * 128].astype(F32)
    for q in range(NQ):
        for half in range(2):
            w = (q * 2 + half) * 2
            b0, b1 = bs[w * 32:w * 32 + 32, :], bs[w * 32 + 32:w * 32 + 64, :]
            ts[pl.ds(0, 32, stride=2), :] = jnp.where(lane, b0, pltpu.roll(b1, 64, 1))
            ts[pl.ds(1, 32, stride=2), :] = jnp.where(lane, pltpu.roll(b0, 64, 1), b1)
            tb[q, yh, yl, z, :, half * 128:half * 128 + 128] = ts[...].astype(BF16)

    def select(h):
        row = lax.broadcasted_iota(jnp.int32, (1280, 640), 0)
        col = lax.broadcasted_iota(jnp.int32, (1280, 640), 1)
        wi = (col * 1639) >> 16
        w = (wi & 12) + ((wi & 1) << 1) + ((wi >> 1) & 1)
        perm[...] = jnp.where(row == w * 80 + 40 * h + col - 40 * wi, 1.0, 0.0).astype(BF16)
        return jnp.dot(pv_ref[...], perm[...], preferred_element_type=F32).astype(BF16)

    pvs[...] = select(1 - yh)
    pvall[yh] = select(yh)

    pl.semaphore_wait(barrier, len(partners))

    ty_cp, tz_cp, pc_cp, loc_cp = {}, {}, {}, {}
    both = tb.at[2:4, yh, yl, z]
    tz_cp[2, 1] = [send(both, both, tz_s.at[2, 0, i], tz_r.at[2, 0, i], zpeer[i]) for i in (0, 1, 2, 3)]
    for q in range(2):
        mine = tb.at[q, yh, yl, z]
        ty_cp[q] = [send(mine, mine, ty_s.at[q, d], ty_r.at[q, d], ypeer[d]) for d in (0, 2, 1)]
    def start(j):
        src = pc_hbm.at[:, pl.ds(j * 16, 16), :]
        loc_cp[j] = pltpu.make_async_copy(src, pcb.at[j, x, core], loc_sem.at[j])
        loc_cp[j].start()
        pc_cp[j] = [send(src, pcb.at[j, x, core], pc_s.at[j, d], pc_r.at[j, d], xpeer[d]) for d in (0, 2, 1)]

    start(0)
    start(1)
    pv_cp = send(pvs, pvall.at[yh], pv_s, pv_r, ypeer[1])

    def e(q, s):
        if s == 1:
            for cp in ty_cp[q]:
                cp.wait_recv()
        else:
            for cp in tz_cp[q, s - 1]:
                cp.wait_recv()
        near, far = lax.rem(z - (s - 1) + Z, Z), lax.rem(z + s - 1, Z)
        if s < 4:
            a, b = tb.at[q, :, :, near], tb.at[q, :, :, far]
        else:
            a, b = tb.at[q, 0, :, near], tb.at[q, 1, :, far]
        tz_cp[q, s] = [send(a, a, tz_s.at[q, s - 1, 0], tz_r.at[q, s - 1, 0], zpeer[0]),
                       send(b, b, tz_s.at[q, s - 1, 1], tz_r.at[q, s - 1, 1], zpeer[1])]

    def a():
        for cp in tz_cp[2, 1]:
            cp.wait_recv()
        near, far = lax.rem(z + Z - 2, Z), lax.rem(z + 2, Z)
        n3, f3 = tb.at[2:4, yh, yl, near], tb.at[2:4, yh, yl, far]
        n4, f4 = tb.at[2, yh, yl, near], tb.at[3, yh, yl, far]
        tz_cp[2, 2] = [send(t, t, tz_s.at[2, 1, i], tz_r.at[2, 1, i], zpeer[i]) for i, t in enumerate((n3, f3, n4, f4))]

    def b(q):
        if q == 2:
            for cp in tz_cp[2, 2]:
                cp.wait_recv()
        mine = tb.at[q, yh, yl]
        ty_cp[q] = [send(mine, mine, ty_s.at[q, d], ty_r.at[q, d], ypeer[d]) for d in (0, 2)]

    def c(q):
        for cp in ty_cp[q]:
            cp.wait_recv()
        below, above = lax.rem(y + 3, 4), lax.rem(y + 1, 4)
        lo = tb.at[q, below // 2, lax.rem(below, 2), 0:4]
        hi = tb.at[q, above // 2, lax.rem(above, 2), 4:8]
        ty_cp[q] = [send(lo, lo, ty_s.at[q, 1], ty_r.at[q, 1], ypeer[0]),
                    send(hi, hi, ty_s.at[q, 3], ty_r.at[q, 3], ypeer[2])]

    def g(q):
        for cp in ty_cp[q]:
            cp.wait_recv()

    def f(q):
        for cp in tz_cp[q, 4]:
            cp.wait_recv()

    sib_cp = {}

    def p2(j):
        loc_cp[j].wait()
        for cp in pc_cp[j]:
            cp.wait_recv()
        sib_cp[j] = send(pcb.at[j, :, core], pcb.at[j, :, core], sib_s.at[j], sib_r.at[j], sibling)

    low = lax.broadcasted_iota(jnp.int32, (80, 128), 1) < 64
    pend = []
    parts = [(i, c) for i in range(2) for c in range(8)]

    def relay(u, some):
        slot, j, par = u
        for i, c in some:
            c0 = jnp.concatenate([ys[par, i, wp, pl.ds(2 * c, 40, stride=16), :] for wp in range(2)], 0).astype(BF16)
            c1 = jnp.concatenate([ys[par, i, wp, pl.ds(2 * c + 1, 40, stride=16), :] for wp in range(2)], 0).astype(BF16)
            at = slot * 320 + i * 160
            xs[at:at + 80, c * 128:c * 128 + 128] = jnp.where(low, c0, pltpu.roll(c1, 64, 1))
            xs[at + 80:at + 160, c * 128:c * 128 + 128] = jnp.where(low, pltpu.roll(c0, 64, 1), c1)

    def finish(u):
        slot, j, par = u
        if slot == 3:
            t = jnp.dot(pvc[:, 960:1280], xs[960:1280, :], preferred_element_type=F32)
            acc[j] = t.reshape(8, 2, 16, 1024)
        elif slot == 2:
            t = jnp.dot(pvc[:, 0:960], xs[0:960, :], preferred_element_type=F32)
            acc[j] += t.reshape(8, 2, 16, 1024)

    count = [0]

    def r(slot, pair, h, j):
        par = count[0] % 2
        count[0] += 1
        last = pend.pop() if pend else None
        for i in range(2):
            rhs = tb[pair * 2 + i, h].reshape(1024, 256)
            for m in range(2):
                prod = jnp.dot(pcb[j, 2 * m:2 * m + 2].reshape(320, 1024), rhs, preferred_element_type=F32)
                for wp in range(2):
                    ys[par, i, wp, m * 320:m * 320 + 320] = prod[:, wp * 128:wp * 128 + 128]
                if last:
                    at = (i * 2 + m) * 4
                    relay(last, parts[at:at + 4])
        if last:
            finish(last)
        pend.append((slot, j, par))

    def flush():
        u = pend.pop()
        relay(u, parts)
        finish(u)

    d2_cp = {}

    def d(j):
        d2_cp[j] = send(acc.at[j, :, 1 - core], rbuf.at[j], d2_s.at[j], d2_r.at[j], sibling)

    o_cp = {}
    who = [lax.rem(x + dx, 4) + 4 * yh for dx in (1, 2, 3)] + [lax.rem(x + dx, 4) + 4 * (1 - yh) for dx in (0, 1, 2, 3)]
    me = x + 4 * yh

    def s(j):
        d2_cp[j].wait_recv()
        sbuf[j] = (acc[j, :, core] + rbuf[j]).astype(BF16)
        o_cp[j] = [send(sbuf.at[j, who[i]], obuf.at[j, i], o_s.at[j, i], o_r.at[j, i], opeer[i]) for i in range(7)]

    def o(j):
        for cp in o_cp[j]:
            cp.wait_recv()
        total = acc[j, me, core] + rbuf[j, me]
        for i in range(7):
            total = total + obuf[j, i].astype(F32)
        out_ref[:, j * 1024:(j + 1) * 1024] = total.astype(BF16)

    e(0, 1)
    e(1, 1)
    a()
    e(0, 2)
    start(2)
    b(2)
    b(3)
    e(1, 2)
    p2(0)
    e(0, 3)
    start(3)
    p2(1)
    e(1, 3)
    c(2)
    pv_cp.wait_recv()
    e(0, 4)
    c(3)
    e(1, 4)
    p2(2)
    for i, (h, at) in enumerate(((0, 0), (1, 0), (1 - yh, 320), (yh, 320))):
        pvc[:, i * 320:i * 320 + 320] = pvall[h, :, at:at + 320]
    for j in range(NJ):
        if j == 2:
            p2(3)
        sib_cp[j].wait_recv()
        r(3, 1, yh, j)
    f(0)
    f(1)
    for j in range(NJ):
        r(0, 0, 0, j)
        if j:
            d(j - 1)
        r(1, 0, 1, j)
        if j == 0:
            g(2)
            g(3)
        r(2, 1, 1 - yh, j)
        if j:
            s(j - 1)
    flush()
    d(NJ - 1)
    o(0)
    s(NJ - 1)
    for j in range(1, NJ):
        o(j)
    for cp in sent:
        cp.wait_send()


def body(trial, pair_cond, pair_val):
    dma = pltpu.SemaphoreType.DMA
    vmem = pl.BlockSpec(memory_space=pltpu.VMEM)
    return pl.pallas_call(
        kernel,
        out_shape=jax.ShapeDtypeStruct((16, 4096), BF16),
        in_specs=[vmem, pl.BlockSpec(memory_space=pl.ANY), vmem],
        out_specs=vmem,
        scratch_shapes=[
            pltpu.VMEM((NJ, 4, 2, 5, 16, 1024), BF16),
            pltpu.VMEM((NQ, 2, 2, Z, 64, 256), BF16),
            pltpu.VMEM((256, 640), BF16),
            pltpu.VMEM((2, 256, 640), BF16),
            pltpu.VMEM((256, 1280), BF16),
            pltpu.VMEM((1280, 640), BF16),
            pltpu.VMEM((512, 128), F32),
            pltpu.VMEM((64, 128), F32),
            pltpu.VMEM((2, 2, 2, 640, 128), F32),
            pltpu.VMEM((1280, 1024), BF16),
            pltpu.VMEM((NJ, 8, 2, 16, 1024), F32),
            pltpu.VMEM((NJ, 8, 16, 1024), F32),
            pltpu.VMEM((NJ, 8, 16, 1024), BF16),
            pltpu.VMEM((NJ, 7, 16, 1024), BF16),
            dma((NJ,)), dma((NJ, 4)), dma((NJ, 4)), dma((NJ,)), dma((NJ,)),
            dma((NQ, 4)), dma((NQ, 4)), dma((NQ, 4, 4)), dma((NQ, 4, 4)), dma(()), dma(()),
            dma((NJ,)), dma((NJ,)), dma((NJ, 7)), dma((NJ, 7)),
        ],
        compiler_params=pltpu.CompilerParams(
            collective_id=0, has_side_effects=True, vmem_limit_bytes=56 << 20
        ),
    )(trial, pair_cond, pair_val)


def solution(mesh):
    in_specs = (P("val", "cond"), P("val", "cond", None), P(None, "val"))
    return jax.shard_map(body, mesh=mesh, in_specs=in_specs, out_specs=P("val", "cond"), check_vma=False)
```

```python
import jax
import jax.numpy as jnp
from jax import lax
from jax.experimental import pallas as pl
from jax.experimental.pallas import tpu as pltpu
from jax.sharding import PartitionSpec as P

MESH = pl.DeviceIdType.MESH
F32, BF16 = jnp.float32, jnp.bfloat16
NQ = 4
NJ = 4
Z = 8


def device(x, y, z, core):
    x, y, z = lax.rem(x + 4, 4), lax.rem(y + 4, 4), lax.rem(z + Z, Z)
    return {"val": (y // 2) * 8 + x * 2 + core, "cond": lax.rem(y, 2) * Z + z}


def kernel(trial_ref, pc_hbm, pv_ref, out_ref, pcb, tb, pvs, pvall, pvc, perm, bs, ts, ys, xs, acc,
           rbuf, sbuf, obuf, loc_sem, pc_s, pc_r, sib_s, sib_r, ty_s, ty_r, tz_s, tz_r, pv_s, pv_r,
           d2_s, d2_r, o_s, o_r):
    val, cond = lax.axis_index("val"), lax.axis_index("cond")
    yh, yl, z = val // 8, cond // Z, lax.rem(cond, Z)
    x, core, y = lax.rem(val, 8) // 2, lax.rem(val, 2), (val // 8) * 2 + cond // Z
    sibling = device(x, y, z, 1 - core)
    xpeer = [device(x + d, y, z, core) for d in (1, 2, 3)]
    ypeer = [device(x, y + d, z, core) for d in (1, 2, 3)]
    zpeer = [device(x, y, z + d, core) for d in (1, -1, 2, -2)]
    opeer = xpeer + [device(x + d, y + 2, z, core) for d in (0, 1, 2, 3)]
    partners = [sibling] + xpeer + ypeer + zpeer

    barrier = pltpu.get_barrier_semaphore()
    for p in partners:
        pl.semaphore_signal(barrier, 1, device_id=p, device_id_type=MESH)
    sent = []

    def send(src, dst, s, r, to):
        cp = pltpu.make_async_remote_copy(src, dst, s, r, device_id=to, device_id_type=MESH)
        cp.start()
        sent.append(cp)
        return cp

    lane = lax.broadcasted_iota(jnp.int32, (32, 128), 1) < 64
    for i in range(32):
        bs[pl.ds(i, 16, stride=32), :] = trial_ref[:, i * 128:(i + 1) * 128].astype(F32)
    for q in range(NQ):
        for half in range(2):
            w = (q * 2 + half) * 2
            b0, b1 = bs[w * 32:w * 32 + 32, :], bs[w * 32 + 32:w * 32 + 64, :]
            ts[pl.ds(0, 32, stride=2), :] = jnp.where(lane, b0, pltpu.roll(b1, 64, 1))
            ts[pl.ds(1, 32, stride=2), :] = jnp.where(lane, pltpu.roll(b0, 64, 1), b1)
            tb[q, yh, yl, z, :, half * 128:half * 128 + 128] = ts[...].astype(BF16)

    def select(h):
        row = lax.broadcasted_iota(jnp.int32, (1280, 640), 0)
        col = lax.broadcasted_iota(jnp.int32, (1280, 640), 1)
        wi = (col * 1639) >> 16
        w = (wi & 12) + ((wi & 1) << 1) + ((wi >> 1) & 1)
        perm[...] = jnp.where(row == w * 80 + 40 * h + col - 40 * wi, 1.0, 0.0).astype(BF16)
        return jnp.dot(pv_ref[...], perm[...], preferred_element_type=F32).astype(BF16)

    pvs[...] = select(1 - yh)
    pvall[yh] = select(yh)

    pl.semaphore_wait(barrier, len(partners))

    ty_cp, tz_cp, pc_cp, loc_cp = {}, {}, {}, {}
    both = tb.at[2:4, yh, yl, z]
    tz_cp[2, 1] = [send(both, both, tz_s.at[2, 0, i], tz_r.at[2, 0, i], zpeer[i]) for i in (0, 1, 2, 3)]
    for q in range(2):
        mine = tb.at[q, yh, yl, z]
        ty_cp[q] = [send(mine, mine, ty_s.at[q, d], ty_r.at[q, d], ypeer[d]) for d in (0, 2, 1)]
    def start(j):
        src = pc_hbm.at[:, pl.ds(j * 16, 16), :]
        loc_cp[j] = pltpu.make_async_copy(src, pcb.at[j, x, core], loc_sem.at[j])
        loc_cp[j].start()
        pc_cp[j] = [send(src, pcb.at[j, x, core], pc_s.at[j, d], pc_r.at[j, d], xpeer[d]) for d in (0, 2, 1)]

    start(0)
    start(1)
    pv_cp = send(pvs, pvall.at[yh], pv_s, pv_r, ypeer[1])

    def e(q, s):
        if s == 1:
            for cp in ty_cp[q]:
                cp.wait_recv()
        else:
            for cp in tz_cp[q, s - 1]:
                cp.wait_recv()
        near, far = lax.rem(z - (s - 1) + Z, Z), lax.rem(z + s - 1, Z)
        if s < 4:
            a, b = tb.at[q, :, :, near], tb.at[q, :, :, far]
        else:
            a, b = tb.at[q, 0, :, near], tb.at[q, 1, :, far]
        tz_cp[q, s] = [send(a, a, tz_s.at[q, s - 1, 0], tz_r.at[q, s - 1, 0], zpeer[0]),
                       send(b, b, tz_s.at[q, s - 1, 1], tz_r.at[q, s - 1, 1], zpeer[1])]

    def a():
        for cp in tz_cp[2, 1]:
            cp.wait_recv()
        near, far = lax.rem(z + Z - 2, Z), lax.rem(z + 2, Z)
        n3, f3 = tb.at[2:4, yh, yl, near], tb.at[2:4, yh, yl, far]
        n4, f4 = tb.at[2, yh, yl, near], tb.at[3, yh, yl, far]
        tz_cp[2, 2] = [send(t, t, tz_s.at[2, 1, i], tz_r.at[2, 1, i], zpeer[i]) for i, t in enumerate((n3, f3, n4, f4))]

    def b(q):
        if q == 2:
            for cp in tz_cp[2, 2]:
                cp.wait_recv()
        mine = tb.at[q, yh, yl]
        ty_cp[q] = [send(mine, mine, ty_s.at[q, d], ty_r.at[q, d], ypeer[d]) for d in (0, 2)]

    def c(q):
        for cp in ty_cp[q]:
            cp.wait_recv()
        below, above = lax.rem(y + 3, 4), lax.rem(y + 1, 4)
        lo = tb.at[q, below // 2, lax.rem(below, 2), 0:4]
        hi = tb.at[q, above // 2, lax.rem(above, 2), 4:8]
        ty_cp[q] = [send(lo, lo, ty_s.at[q, 1], ty_r.at[q, 1], ypeer[0]),
                    send(hi, hi, ty_s.at[q, 3], ty_r.at[q, 3], ypeer[2])]

    def g(q):
        for cp in ty_cp[q]:
            cp.wait_recv()

    def f(q):
        for cp in tz_cp[q, 4]:
            cp.wait_recv()

    sib_cp = {}

    def p2(j):
        loc_cp[j].wait()
        for cp in pc_cp[j]:
            cp.wait_recv()
        sib_cp[j] = send(pcb.at[j, :, core], pcb.at[j, :, core], sib_s.at[j], sib_r.at[j], sibling)

    low = lax.broadcasted_iota(jnp.int32, (80, 128), 1) < 64
    pend = []
    parts = [(i, c) for i in range(2) for c in range(8)]

    def relay(u, some):
        slot, j, par = u
        for i, c in some:
            c0 = jnp.concatenate([ys[par, i, wp, pl.ds(2 * c, 40, stride=16), :] for wp in range(2)], 0).astype(BF16)
            c1 = jnp.concatenate([ys[par, i, wp, pl.ds(2 * c + 1, 40, stride=16), :] for wp in range(2)], 0).astype(BF16)
            at = slot * 320 + i * 160
            xs[at:at + 80, c * 128:c * 128 + 128] = jnp.where(low, c0, pltpu.roll(c1, 64, 1))
            xs[at + 80:at + 160, c * 128:c * 128 + 128] = jnp.where(low, pltpu.roll(c0, 64, 1), c1)

    def finish(u):
        slot, j, par = u
        if slot == 3:
            t = jnp.dot(pvc[:, 960:1280], xs[960:1280, :], preferred_element_type=F32)
            acc[j] = t.reshape(8, 2, 16, 1024)
        elif slot == 2:
            t = jnp.dot(pvc[:, 0:960], xs[0:960, :], preferred_element_type=F32)
            acc[j] += t.reshape(8, 2, 16, 1024)

    count = [0]

    def r(slot, pair, h, j, between=None):
        par = count[0] % 2
        count[0] += 1
        last = pend.pop() if pend else None
        for i in range(2):
            if i and between:
                between()
            rhs = tb[pair * 2 + i, h].reshape(1024, 256)
            if last:
                relay(last, parts[i * 8:i * 8 + 8])
            prod = jnp.dot(pcb[j].reshape(640, 1024), rhs, preferred_element_type=F32)
            for wp in range(2):
                ys[par, i, wp] = prod[:, wp * 128:wp * 128 + 128]
        if last:
            finish(last)
        pend.append((slot, j, par))

    def flush():
        u = pend.pop()
        relay(u, parts)
        finish(u)

    d2_cp = {}

    def d(j):
        d2_cp[j] = send(acc.at[j, :, 1 - core], rbuf.at[j], d2_s.at[j], d2_r.at[j], sibling)

    o_cp = {}
    who = [lax.rem(x + dx, 4) + 4 * yh for dx in (1, 2, 3)] + [lax.rem(x + dx, 4) + 4 * (1 - yh) for dx in (0, 1, 2, 3)]
    me = x + 4 * yh

    def s(j):
        d2_cp[j].wait_recv()
        sbuf[j] = (acc[j, :, core] + rbuf[j]).astype(BF16)
        o_cp[j] = [send(sbuf.at[j, who[i]], obuf.at[j, i], o_s.at[j, i], o_r.at[j, i], opeer[i]) for i in (5, 1, 4, 6, 3, 0, 2)]

    def o(j):
        for cp in o_cp[j]:
            cp.wait_recv()
        total = acc[j, me, core] + rbuf[j, me]
        for i in range(7):
            total = total + obuf[j, i].astype(F32)
        out_ref[:, j * 1024:(j + 1) * 1024] = total.astype(BF16)

    e(0, 1)
    e(1, 1)
    a()
    e(0, 2)
    start(2)
    b(2)
    b(3)
    e(1, 2)
    p2(0)
    e(0, 3)
    start(3)
    p2(1)
    e(1, 3)
    c(2)
    pv_cp.wait_recv()
    e(0, 4)
    c(3)
    e(1, 4)
    p2(2)
    for i, (h, at) in enumerate(((0, 0), (1, 0), (1 - yh, 320), (yh, 320))):
        pvc[:, i * 320:i * 320 + 320] = pvall[h, :, at:at + 320]
    for j in range(NJ):
        if j == 1:
            p2(3)
        sib_cp[j].wait_recv()
        r(3, 1, yh, j)
    f(0)
    for j in range(NJ):
        r(0, 0, 0, j, None if j else lambda: f(1))
        if j:
            d(j - 1)
        r(1, 0, 1, j)
        if j == 0:
            g(2)
            g(3)
        r(2, 1, 1 - yh, j)
        if j:
            s(j - 1)
    flush()
    d(NJ - 1)
    o(0)
    s(NJ - 1)
    for j in range(1, NJ):
        o(j)
    for cp in sent:
        cp.wait_send()


def body(trial, pair_cond, pair_val):
    dma = pltpu.SemaphoreType.DMA
    vmem = pl.BlockSpec(memory_space=pltpu.VMEM)
    return pl.pallas_call(
        kernel,
        out_shape=jax.ShapeDtypeStruct((16, 4096), BF16),
        in_specs=[vmem, pl.BlockSpec(memory_space=pl.ANY), vmem],
        out_specs=vmem,
        scratch_shapes=[
            pltpu.VMEM((NJ, 4, 2, 5, 16, 1024), BF16),
            pltpu.VMEM((NQ, 2, 2, Z, 64, 256), BF16),
            pltpu.VMEM((256, 640), BF16),
            pltpu.VMEM((2, 256, 640), BF16),
            pltpu.VMEM((256, 1280), BF16),
            pltpu.VMEM((1280, 640), BF16),
            pltpu.VMEM((512, 128), F32),
            pltpu.VMEM((64, 128), F32),
            pltpu.VMEM((2, 2, 2, 640, 128), F32),
            pltpu.VMEM((1280, 1024), BF16),
            pltpu.VMEM((NJ, 8, 2, 16, 1024), F32),
            pltpu.VMEM((NJ, 8, 16, 1024), F32),
            pltpu.VMEM((NJ, 8, 16, 1024), BF16),
            pltpu.VMEM((NJ, 7, 16, 1024), BF16),
            dma((NJ,)), dma((NJ, 4)), dma((NJ, 4)), dma((NJ,)), dma((NJ,)),
            dma((NQ, 4)), dma((NQ, 4)), dma((NQ, 4, 4)), dma((NQ, 4, 4)), dma(()), dma(()),
            dma((NJ,)), dma((NJ,)), dma((NJ, 7)), dma((NJ, 7)),
        ],
        compiler_params=pltpu.CompilerParams(
            collective_id=0, has_side_effects=True, vmem_limit_bytes=56 << 20
        ),
    )(trial, pair_cond, pair_val)


def solution(mesh):
    in_specs = (P("val", "cond"), P("val", "cond", None), P(None, "val"))
    return jax.shard_map(body, mesh=mesh, in_specs=in_specs, out_specs=P("val", "cond"), check_vma=False)
```

```python
import jax
import jax.numpy as jnp
from jax import lax
from jax.experimental import pallas as pl
from jax.experimental.pallas import tpu as pltpu
from jax.sharding import PartitionSpec as P

MESH = pl.DeviceIdType.MESH
F32, BF16 = jnp.float32, jnp.bfloat16
NQ = 4
NJ = 4
Z = 8


def device(x, y, z, core):
    x, y, z = lax.rem(x + 4, 4), lax.rem(y + 4, 4), lax.rem(z + Z, Z)
    return {"val": (y // 2) * 8 + x * 2 + core, "cond": lax.rem(y, 2) * Z + z}


def kernel(trial_ref, pc_hbm, pv_ref, out_ref, pcb, tb, pvs, pvall, pvc, perm, bs, ts, ys, xs, acc,
           rbuf, sbuf, obuf, loc_sem, pc_s, pc_r, sib_s, sib_r, ty_s, ty_r, tz_s, tz_r, pv_s, pv_r,
           d2_s, d2_r, o_s, o_r):
    val, cond = lax.axis_index("val"), lax.axis_index("cond")
    yh, yl, z = val // 8, cond // Z, lax.rem(cond, Z)
    x, core, y = lax.rem(val, 8) // 2, lax.rem(val, 2), (val // 8) * 2 + cond // Z
    sibling = device(x, y, z, 1 - core)
    xpeer = [device(x + d, y, z, core) for d in (1, 2, 3)]
    ypeer = [device(x, y + d, z, core) for d in (1, 2, 3)]
    zpeer = [device(x, y, z + d, core) for d in (1, -1, 2, -2)]
    opeer = xpeer + [device(x + d, y + 2, z, core) for d in (0, 1, 2, 3)]
    partners = [sibling] + xpeer + ypeer + zpeer

    barrier = pltpu.get_barrier_semaphore()
    for p in partners:
        pl.semaphore_signal(barrier, 1, device_id=p, device_id_type=MESH)
    sent = []

    def send(src, dst, s, r, to):
        cp = pltpu.make_async_remote_copy(src, dst, s, r, device_id=to, device_id_type=MESH)
        cp.start()
        sent.append(cp)
        return cp

    lane = lax.broadcasted_iota(jnp.int32, (32, 128), 1) < 64
    for i in range(32):
        bs[pl.ds(i, 16, stride=32), :] = trial_ref[:, i * 128:(i + 1) * 128].astype(F32)
    for q in range(NQ):
        for half in range(2):
            w = (q * 2 + half) * 2
            b0, b1 = bs[w * 32:w * 32 + 32, :], bs[w * 32 + 32:w * 32 + 64, :]
            ts[pl.ds(0, 32, stride=2), :] = jnp.where(lane, b0, pltpu.roll(b1, 64, 1))
            ts[pl.ds(1, 32, stride=2), :] = jnp.where(lane, pltpu.roll(b0, 64, 1), b1)
            tb[q, yh, yl, z, :, half * 128:half * 128 + 128] = ts[...].astype(BF16)

    def select(h):
        row = lax.broadcasted_iota(jnp.int32, (1280, 640), 0)
        col = lax.broadcasted_iota(jnp.int32, (1280, 640), 1)
        wi = (col * 1639) >> 16
        w = (wi & 12) + ((wi & 1) << 1) + ((wi >> 1) & 1)
        perm[...] = jnp.where(row == w * 80 + 40 * h + col - 40 * wi, 1.0, 0.0).astype(BF16)
        return jnp.dot(pv_ref[...], perm[...], preferred_element_type=F32).astype(BF16)

    pvs[...] = select(1 - yh)
    pvall[yh] = select(yh)

    pl.semaphore_wait(barrier, len(partners))

    ty_cp, tz_cp, pc_cp, loc_cp = {}, {}, {}, {}
    for q in range(2):
        mine = tb.at[q, yh, yl, z]
        ty_cp[q] = [send(mine, mine, ty_s.at[q, d], ty_r.at[q, d], ypeer[d]) for d in (0, 2, 1)]
    both = tb.at[2:4, yh, yl, z]
    tz_cp[2, 1] = [send(both, both, tz_s.at[2, 0, i], tz_r.at[2, 0, i], zpeer[i]) for i in (0, 1, 2, 3)]
    def start(j):
        src = pc_hbm.at[:, pl.ds(j * 16, 16), :]
        loc_cp[j] = pltpu.make_async_copy(src, pcb.at[j, x, core], loc_sem.at[j])
        loc_cp[j].start()
        pc_cp[j] = [send(src, pcb.at[j, x, core], pc_s.at[j, d], pc_r.at[j, d], xpeer[d]) for d in (0, 2, 1)]

    start(0)
    start(1)
    pv_cp = send(pvs, pvall.at[yh], pv_s, pv_r, ypeer[1])

    def e(q, s):
        if s == 1:
            for cp in ty_cp[q]:
                cp.wait_recv()
        else:
            for cp in tz_cp[q, s - 1]:
                cp.wait_recv()
        near, far = lax.rem(z - (s - 1) + Z, Z), lax.rem(z + s - 1, Z)
        if s < 4:
            a, b = tb.at[q, :, :, near], tb.at[q, :, :, far]
        else:
            a, b = tb.at[q, 0, :, near], tb.at[q, 1, :, far]
        tz_cp[q, s] = [send(a, a, tz_s.at[q, s - 1, 0], tz_r.at[q, s - 1, 0], zpeer[0]),
                       send(b, b, tz_s.at[q, s - 1, 1], tz_r.at[q, s - 1, 1], zpeer[1])]

    def a():
        for cp in tz_cp[2, 1]:
            cp.wait_recv()
        near, far = lax.rem(z + Z - 2, Z), lax.rem(z + 2, Z)
        n3, f3 = tb.at[2:4, yh, yl, near], tb.at[2:4, yh, yl, far]
        n4, f4 = tb.at[2, yh, yl, near], tb.at[3, yh, yl, far]
        tz_cp[2, 2] = [send(t, t, tz_s.at[2, 1, i], tz_r.at[2, 1, i], zpeer[i]) for i, t in enumerate((n3, f3, n4, f4))]

    def b(q):
        if q == 2:
            for cp in tz_cp[2, 2]:
                cp.wait_recv()
        mine = tb.at[q, yh, yl]
        ty_cp[q] = [send(mine, mine, ty_s.at[q, d], ty_r.at[q, d], ypeer[d]) for d in (0, 2)]

    def c(q):
        for cp in ty_cp[q]:
            cp.wait_recv()
        below, above = lax.rem(y + 3, 4), lax.rem(y + 1, 4)
        lo = tb.at[q, below // 2, lax.rem(below, 2), 0:4]
        hi = tb.at[q, above // 2, lax.rem(above, 2), 4:8]
        ty_cp[q] = [send(lo, lo, ty_s.at[q, 1], ty_r.at[q, 1], ypeer[0]),
                    send(hi, hi, ty_s.at[q, 3], ty_r.at[q, 3], ypeer[2])]

    def g(q):
        for cp in ty_cp[q]:
            cp.wait_recv()

    def f(q):
        for cp in tz_cp[q, 4]:
            cp.wait_recv()

    sib_cp = {}

    def p2(j):
        loc_cp[j].wait()
        for cp in pc_cp[j]:
            cp.wait_recv()
        sib_cp[j] = send(pcb.at[j, :, core], pcb.at[j, :, core], sib_s.at[j], sib_r.at[j], sibling)

    low = lax.broadcasted_iota(jnp.int32, (80, 128), 1) < 64
    pend = []
    parts = [(i, c) for i in range(2) for c in range(8)]

    def relay(u, some):
        slot, j, par = u
        for i, c in some:
            c0 = jnp.concatenate([ys[par, i, wp, pl.ds(2 * c, 40, stride=16), :] for wp in range(2)], 0).astype(BF16)
            c1 = jnp.concatenate([ys[par, i, wp, pl.ds(2 * c + 1, 40, stride=16), :] for wp in range(2)], 0).astype(BF16)
            at = slot * 320 + i * 160
            xs[at:at + 80, c * 128:c * 128 + 128] = jnp.where(low, c0, pltpu.roll(c1, 64, 1))
            xs[at + 80:at + 160, c * 128:c * 128 + 128] = jnp.where(low, pltpu.roll(c0, 64, 1), c1)

    def finish(u):
        slot, j, par = u
        if slot == 3:
            t = jnp.dot(pvc[:, 960:1280], xs[960:1280, :], preferred_element_type=F32)
            acc[j] = t.reshape(8, 2, 16, 1024)
        elif slot == 2:
            t = jnp.dot(pvc[:, 0:960], xs[0:960, :], preferred_element_type=F32)
            acc[j] += t.reshape(8, 2, 16, 1024)

    count = [0]

    def r(slot, pair, h, j, between=None):
        par = count[0] % 2
        count[0] += 1
        last = pend.pop() if pend else None
        for i in range(2):
            if i and between:
                between()
            rhs = tb[pair * 2 + i, h].reshape(1024, 256)
            if last:
                relay(last, parts[i * 8:i * 8 + 8])
            prod = jnp.dot(pcb[j].reshape(640, 1024), rhs, preferred_element_type=F32)
            for wp in range(2):
                ys[par, i, wp] = prod[:, wp * 128:wp * 128 + 128]
        if last:
            finish(last)
        pend.append((slot, j, par))

    def flush():
        u = pend.pop()
        relay(u, parts)
        finish(u)

    d2_cp = {}

    def d(j):
        d2_cp[j] = send(acc.at[j, :, 1 - core], rbuf.at[j], d2_s.at[j], d2_r.at[j], sibling)

    o_cp = {}
    who = [lax.rem(x + dx, 4) + 4 * yh for dx in (1, 2, 3)] + [lax.rem(x + dx, 4) + 4 * (1 - yh) for dx in (0, 1, 2, 3)]
    me = x + 4 * yh

    def s(j):
        d2_cp[j].wait_recv()
        sbuf[j] = (acc[j, :, core] + rbuf[j]).astype(BF16)
        o_cp[j] = [send(sbuf.at[j, who[i]], obuf.at[j, i], o_s.at[j, i], o_r.at[j, i], opeer[i]) for i in (5, 1, 4, 6, 3, 0, 2)]

    def o(j):
        for cp in o_cp[j]:
            cp.wait_recv()
        total = acc[j, me, core] + rbuf[j, me]
        for i in range(7):
            total = total + obuf[j, i].astype(F32)
        out_ref[:, j * 1024:(j + 1) * 1024] = total.astype(BF16)

    e(0, 1)
    e(1, 1)
    a()
    e(0, 2)
    start(2)
    b(2)
    b(3)
    e(1, 2)
    p2(0)
    e(0, 3)
    start(3)
    p2(1)
    e(1, 3)
    c(2)
    pv_cp.wait_recv()
    e(0, 4)
    c(3)
    e(1, 4)
    p2(2)
    for i, (h, at) in enumerate(((0, 0), (1, 0), (1 - yh, 320), (yh, 320))):
        pvc[:, i * 320:i * 320 + 320] = pvall[h, :, at:at + 320]
    for j in range(NJ):
        if j == 1:
            p2(3)
        sib_cp[j].wait_recv()
        r(3, 1, yh, j)
    f(0)
    for j in range(NJ):
        r(0, 0, 0, j, None if j else lambda: f(1))
        if j:
            d(j - 1)
        r(1, 0, 1, j)
        if j == 0:
            g(2)
            g(3)
        r(2, 1, 1 - yh, j)
        if j:
            s(j - 1)
    flush()
    d(NJ - 1)
    o(0)
    s(NJ - 1)
    for j in range(1, NJ):
        o(j)
    for cp in sent:
        cp.wait_send()


def body(trial, pair_cond, pair_val):
    dma = pltpu.SemaphoreType.DMA
    vmem = pl.BlockSpec(memory_space=pltpu.VMEM)
    return pl.pallas_call(
        kernel,
        out_shape=jax.ShapeDtypeStruct((16, 4096), BF16),
        in_specs=[vmem, pl.BlockSpec(memory_space=pl.ANY), vmem],
        out_specs=vmem,
        scratch_shapes=[
            pltpu.VMEM((NJ, 4, 2, 5, 16, 1024), BF16),
            pltpu.VMEM((NQ, 2, 2, Z, 64, 256), BF16),
            pltpu.VMEM((256, 640), BF16),
            pltpu.VMEM((2, 256, 640), BF16),
            pltpu.VMEM((256, 1280), BF16),
            pltpu.VMEM((1280, 640), BF16),
            pltpu.VMEM((512, 128), F32),
            pltpu.VMEM((64, 128), F32),
            pltpu.VMEM((2, 2, 2, 640, 128), F32),
            pltpu.VMEM((1280, 1024), BF16),
            pltpu.VMEM((NJ, 8, 2, 16, 1024), F32),
            pltpu.VMEM((NJ, 8, 16, 1024), F32),
            pltpu.VMEM((NJ, 8, 16, 1024), BF16),
            pltpu.VMEM((NJ, 7, 16, 1024), BF16),
            dma((NJ,)), dma((NJ, 4)), dma((NJ, 4)), dma((NJ,)), dma((NJ,)),
            dma((NQ, 4)), dma((NQ, 4)), dma((NQ, 4, 4)), dma((NQ, 4, 4)), dma(()), dma(()),
            dma((NJ,)), dma((NJ,)), dma((NJ, 7)), dma((NJ, 7)),
        ],
        compiler_params=pltpu.CompilerParams(
            collective_id=0, has_side_effects=True, vmem_limit_bytes=56 << 20
        ),
    )(trial, pair_cond, pair_val)


def solution(mesh):
    in_specs = (P("val", "cond"), P("val", "cond", None), P(None, "val"))
    return jax.shard_map(body, mesh=mesh, in_specs=in_specs, out_specs=P("val", "cond"), check_vma=False)
```
